32 devices in a mesh: leaf: 4 (over y, x), panel: 8 (over z, core).
Axes of the slice: x: 2, y: 2, z: 4, core: 2. Of those that a mesh axis runs over, the one named last changes fastest.
Arguments:
- right_sides: bfloat16 [3, 12288, 128], P(None, ('leaf', 'panel')), may hold values from -6 to 6
- inverse_low: bfloat16 [12288, 3072], P(('leaf', 'panel')), may hold values from -1 to 1, as said below
- inverse_mid: bfloat16 [12288, 6144], P(('leaf', 'panel')), may hold values from -1 to 1, as said below
- inverse_top: bfloat16 [12288, 12288], P(('leaf', 'panel')), may hold values from -1 to 1, as said below
- update_low: bfloat16 [12288, 3072], P(('leaf', 'panel')), may hold values from -0.109375 to 0.109375
- update_mid: bfloat16 [12288, 6144], P(('leaf', 'panel')), may hold values from -0.078125 to 0.078125
- slots_low: int32 [4, 3072], replicated, may hold values from 0 to 6143, as said below
- slots_mid: int32 [2, 6144], replicated, may hold values from 0 to 12287, as said below
Outputs:
- solutions: bfloat16 [3, 12288, 128], P(None, ('leaf', 'panel'))
The draws below stay inside these ranges and needn't reach their ends.
Inputs may be any that keep to these rules, and one draw needn't show every extreme that they name: `inverse_low`: within each supernode's rows, the block is lower triangular with a unit diagonal. `inverse_mid`: within each supernode's rows, the block is lower triangular with a unit diagonal. `inverse_top`: within each supernode's rows, the block is lower triangular with a unit diagonal. `slots_low`: each row lists 3072 distinct rows of the parent supernode. `slots_mid`: each row lists 6144 distinct rows of the parent supernode.
All inputs are finite; a program needn't handle non-finite values.
Results may differ from the reference program's by a relative error of at most 0.015.
Values may be sent and summed in bfloat16 or wider, within the bound.
No kernel may reach another device: no remote copies, remote signals or barrier semaphores. Data moves between devices by JAX's collectives and lax.ppermute only.
A program may use at most 128 MiB of HBM per device.

```python
import math
import jax
import jax.numpy as jnp
from jax import lax

SEP0 = 3072
VEC = 128
LEVELS = 3
SEP1 = 6144
SEP2 = 12288
ROWS = 12288
NODES = 4
PAIRS = 2


def lower_inverse(key, extent):
    row_at = lax.broadcasted_iota(jnp.int32, (ROWS, extent), 0) % extent
    col_at = lax.broadcasted_iota(jnp.int32, (ROWS, extent), 1)
    random_part = jnp.clip(jax.random.normal(key, (ROWS, extent), jnp.float32), -6.0, 6.0)
    lower_part = jnp.where(col_at < row_at, random_part * (1.0 / math.sqrt(extent)), 0.0)
    return (lower_part + jnp.where(col_at == row_at, 1.0, 0.0)).astype(jnp.bfloat16)


def draw_inverse_low(key, part):
    return lower_inverse(key, SEP0)


def draw_inverse_mid(key, part):
    return lower_inverse(key, SEP1)


def draw_inverse_top(key, part):
    return lower_inverse(key, SEP2)


def parent_slots(key, number, listed, extent):

    def single(subkey):
        first_key, second_key = jax.random.split(subkey)
        middle = 1 + jax.random.permutation(first_key, extent - 2)[:listed - 2]
        chosen = jnp.concatenate([jnp.array([0, extent - 1], jnp.int32), middle.astype(jnp.int32)])
        return jax.random.permutation(second_key, chosen)
    return jax.vmap(single)(jax.random.split(key, number))


def draw_slots_low(key, part):
    return parent_slots(key, NODES, SEP0, SEP1)


def draw_slots_mid(key, part):
    return parent_slots(key, PAIRS, SEP1, SEP2)


def steps_of(stream_key, dims, cuts, least, high):
    def one(dim, parts):
        heights = jax.random.uniform(jax.random.fold_in(jax.random.fold_in(stream_key, 6), dim), (parts,), jnp.float32, least / len(cuts), high / len(cuts))
        return jnp.repeat(jnp.exp(heights), dims[dim] // parts).reshape((-1,) + (1,) * (len(dims) - dim - 1))

    gain = one(*cuts[0])
    for cut in cuts[1:]:
        gain = gain * one(*cut)
    return gain


def normal_values(stream_key, dims, deviation, reach, shards=(), kind=jnp.bfloat16):
    result = deviation * jax.random.normal(stream_key, dims, jnp.float32)
    if shards:
        result = result * steps_of(stream_key, dims, shards, -0.22, 0.18)
    return jnp.clip(result, -reach, reach).astype(kind)


def setup_inputs(seed: int = 0) -> dict:
    key_of = jax.random.split(jax.random.key(seed), 9)
    return {
        "right_sides": normal_values(key_of[0], (LEVELS, ROWS, VEC), 1.0, 6.0, ((1, 32),)),
        "inverse_low": draw_inverse_low(jax.random.fold_in(key_of[8], 71), 0),
        "inverse_mid": draw_inverse_mid(jax.random.fold_in(key_of[8], 71), 0),
        "inverse_top": draw_inverse_top(jax.random.fold_in(key_of[8], 71), 0),
        "update_low": normal_values(key_of[4], (ROWS, SEP0), SEP0 ** -0.5, 0.109375, ((0, 32),)),
        "update_mid": normal_values(key_of[5], (ROWS, SEP1), SEP1 ** -0.5, 0.078125, ((0, 32),)),
        "slots_low": draw_slots_low(jax.random.fold_in(key_of[8], 71), 0),
        "slots_mid": draw_slots_mid(jax.random.fold_in(key_of[8], 71), 0),
    }


def reference(right_sides, inverse_low, inverse_mid, inverse_top, update_low, update_mid, slots_low, slots_mid):
    inverses = (inverse_low, inverse_mid, inverse_top)
    updates = (update_low, update_mid)
    lists = (slots_low, slots_mid)
    solved = []
    targets_all = []
    carried = None
    for height_at in range(LEVELS):
        extent = SEP0 * 2 ** height_at
        node_count = ROWS // extent
        if height_at == 0:
            local_rows = right_sides[0]
        else:
            local_rows = (right_sides[height_at].astype(jnp.float32) - carried).astype(jnp.bfloat16)
        blocks = local_rows.reshape(node_count, extent, VEC)
        matrices = inverses[height_at].reshape(node_count, extent, extent)
        solved_now = lax.map(lambda operands: jnp.dot(operands[0], operands[1], preferred_element_type=jnp.float32), (matrices, blocks)).astype(jnp.bfloat16)
        solved.append(solved_now)
        if height_at + 1 < LEVELS:
            update_mats = updates[height_at].reshape(node_count, extent, extent)
            products = lax.map(lambda operands: lax.dot_general(operands[0], operands[1], (((0,), (0,)), ((), ())), preferred_element_type=jnp.float32), (update_mats, solved_now))
            parents = (jnp.arange(node_count, dtype=jnp.int32) // 2) * (2 * extent)
            targets = (lists[height_at].astype(jnp.int32) + parents[:, None]).reshape(-1)
            targets_all.append(targets)
            carried = jax.ops.segment_sum(products.reshape(-1, VEC), targets, num_segments=ROWS)
    results = [None] * LEVELS
    above = None
    for height_at in reversed(range(LEVELS)):
        extent = SEP0 * 2 ** height_at
        node_count = ROWS // extent
        matrices = inverses[height_at].reshape(node_count, extent, extent)
        solved_now = solved[height_at]
        if height_at + 1 < LEVELS:
            update_mats = updates[height_at].reshape(node_count, extent, extent)
            picked = jnp.take(above, targets_all[height_at], axis=0).reshape(node_count, extent, VEC)
            correction = lax.map(lambda operands: jnp.dot(operands[0], operands[1], preferred_element_type=jnp.float32), (update_mats, picked))
            target = (solved_now.astype(jnp.float32) - correction).astype(jnp.bfloat16)
        else:
            target = solved_now
        result_now = lax.map(lambda operands: lax.dot_general(operands[0], operands[1], (((0,), (0,)), ((), ())), preferred_element_type=jnp.float32), (matrices, target))
        above = result_now.astype(jnp.bfloat16).reshape(ROWS, VEC)
        results[height_at] = above
    return jnp.stack(results)
```

```python
import functools

import jax
import jax.numpy as jnp
from jax import lax
from jax.experimental import pallas as pl
from jax.experimental.pallas import tpu as pltpu
from jax.sharding import PartitionSpec as P


AXES = ("leaf", "panel")
CORES = 2
F32 = jnp.float32
BF16 = jnp.bfloat16


def swap_leaf(value, bit_at):
    leaves, panels = lax.axis_size("leaf"), lax.axis_size("panel")
    pairs = [
        (leaf * panels + at, (leaf ^ 1 << bit_at) * panels + at)
        for leaf in range(leaves)
        for at in range(panels)
    ]
    return lax.ppermute(value, AXES, pairs)


def swap_core(value):
    count = lax.axis_size("leaf") * lax.axis_size("panel")
    return lax.ppermute(value, AXES, [(i, i ^ 1) for i in range(count)])


def shift_depth(value, step):
    leaves, panels = lax.axis_size("leaf"), lax.axis_size("panel")
    depth = panels // CORES
    pairs = []
    for leaf in range(leaves):
        for at in range(panels):
            z, core = divmod(at, CORES)
            pairs.append((leaf * panels + at, leaf * panels + (z + step) % depth * CORES + core))
    return lax.ppermute(value, AXES, pairs)


def gather_blocks(block, bits):
    depth = lax.axis_size("panel") // CORES
    held = {(0, 0): block}
    for step in range(1, depth):
        held[0, step] = shift_depth(block, step)
    if bits >= 1:
        for step in range(depth):
            held[1, step] = swap_leaf(held[0, step], 0)
    if bits >= 2:
        for step in range(depth):
            held[2, step] = swap_leaf(held[0, step], 1)
            if step % 2:
                held[3, step] = swap_leaf(held[1, step], 1)
            else:
                held[3, step] = swap_leaf(held[2, step], 0)
    blocks = {}
    for (leaf_diff, step), value in held.items():
        blocks[leaf_diff, step, 0] = value
        blocks[leaf_diff, step, 1] = swap_core(value)
    return blocks


def add(*values):
    total = values[0].astype(F32)
    for value in values[1:]:
        total = total + value.astype(F32)
    return total


def scatter_groups(bits, depth):
    if bits == 0:
        return [[(0, step)] for step in range(depth)]
    if bits == 1:
        return [[(1, step) for step in range(depth)]] + [[(0, step)] for step in range(depth)]
    even, odd = range(0, depth, 2), range(1, depth, 2)
    return [
        [(3, step) for step in even] + [(1, step) for step in even],
        [(3, step) for step in odd] + [(2, step) for step in odd],
        [(2, step) for step in even],
        [(1, step) for step in odd],
    ] + [[(0, step)] for step in range(depth)]


def reduce_blocks(kept, sent, bits):
    depth = lax.axis_size("panel") // CORES
    groups = scatter_groups(bits, depth)
    total = {}
    received = [swap_core(value) for value in sent]
    summed = [add(a, b) for a, b in zip(kept, received)]
    keys = {tuple(keys): value for keys, value in zip(map(tuple, groups), summed)}
    by_first = list(keys.values())
    half = depth // 2
    if bits == 0:
        base = by_first
    elif bits == 1:
        other = swap_leaf(by_first[0].astype(BF16), 0)
        base = [add(by_first[1 + step], other[step : step + 1]) for step in range(depth)]
    else:
        via_low = swap_leaf(by_first[0].astype(BF16), 0)
        via_high = swap_leaf(by_first[1].astype(BF16), 1)
        count = len(range(0, depth, 2))
        even_sum = add(by_first[2], via_low[:count])
        odd_sum = add(by_first[3], via_high[: depth - count])
        even_next = swap_leaf(even_sum.astype(BF16), 1)
        odd_next = swap_leaf(odd_sum.astype(BF16), 0)
        base = []
        for step in range(depth):
            at = step // 2
            if step % 2:
                first, second = via_high[depth - count + at], odd_next[at]
            else:
                first, second = via_low[count + at], even_next[at]
            base.append(add(by_first[4 + step], first[None], second[None]))
    arrived = [shift_depth(base[step].astype(BF16), step) for step in range(1, depth)]
    return add(base[0], *arrived)[0]


def own_place(bits, depth):
    leaf = lax.axis_index("leaf") & (2**bits - 1)
    panel = lax.axis_index("panel")
    return leaf, panel // CORES, panel % CORES


def block_index(place, depth, leaf_diff, step, swap):
    leaf, z, core = place
    return ((leaf ^ leaf_diff) * depth + lax.rem(z + step + depth, depth)) * CORES + (core ^ swap)


def widths(extent, most):
    width = extent
    while width > most and width % 2 == 0 and width // 2 % 128 == 0:
        width //= 2
    return width


def kernel_body(plan, *refs):
    bits_in, bits_out, depth, mode, keys_in, groups = (
        plan["bits_in"], plan["bits_out"], plan["depth"], plan["mode"], plan["keys_in"], plan["groups"],
    )
    refs = list(refs)
    take = lambda count: [refs.pop(0) for _ in range(count)]
    slot_ref = take(1)[0] if mode != "top" else None
    block_refs = take(len(keys_in))
    inverse_ref = take(1)[0]
    update_ref = take(1)[0] if mode != "top" else None
    prior_ref = take(1)[0] if mode == "back" else None
    solved_ref = take(1)[0] if mode == "fwd" else None
    kept_refs = take(len(groups))
    sent_refs = take(len(groups))
    full = take(1)[0]
    inverse = take(1)[0]
    update = take(1)[0] if mode != "top" else None
    wide = take(1)[0] if mode != "top" else None
    narrow = take(1)[0] if mode != "top" else None
    picked = take(1)[0] if mode == "back" else None
    result = take(1)[0]
    in_sem, inverse_sem, update_sem, out_sem = take(4)
    rows = plan["rows"]
    extent = plan["extent"]
    place_in = own_place(bits_in, depth)
    place_out = own_place(bits_out, depth)
    load_width, mul_width = plan["load_width"], plan["mul_width"]

    def start_weights(source, target, sem):
        copies = []
        for at in range(extent // load_width):
            cols = pl.ds(at * load_width, load_width)
            copy = pltpu.make_async_copy(source.at[:, cols], target.at[:, cols], sem.at[at])
            copy.start()
            copies.append(copy)
        return copies

    in_copies = []
    for at, (leaf_diff, step, swap) in enumerate(keys_in):
        index = block_index(place_in, depth, leaf_diff, -step, swap)
        target = full.at[pl.ds(pl.multiple_of(index * rows, rows), rows), :]
        copy = pltpu.make_async_copy(block_refs[at], target, in_sem.at[at])
        copy.start()
        in_copies.append(copy)
    if mode == "back":
        update_copies = start_weights(update_ref, update, update_sem)
        inverse_copies = start_weights(inverse_ref, inverse, inverse_sem)
    else:
        inverse_copies = start_weights(inverse_ref, inverse, inverse_sem)
        update_copies = start_weights(update_ref, update, update_sem) if mode == "fwd" else None

    unroll = 16

    def rowwise(matrix, copies, vector):
        total = None
        for at in range(extent // load_width):
            copies[at].wait()
            cols = pl.ds(at * load_width, load_width)
            term = jnp.dot(matrix[:, cols], vector[cols, :], preferred_element_type=F32)
            total = term if total is None else total + term
        return total

    def colwise(vector_t, matrix, copies, store):
        if copies is not None:
            for copy in copies:
                copy.wait()

        def one(at, carry):
            start = pl.multiple_of(at * mul_width, mul_width)
            product = jnp.dot(vector_t, matrix[:, pl.ds(start, mul_width)], preferred_element_type=F32)
            store(start, product.T)
            return carry

        lax.fori_loop(0, extent // mul_width, one, 0)

    def convert(source, target, count, kind):
        chunk = 512 if count % 512 == 0 else count

        def one(at, carry):
            span = pl.ds(pl.multiple_of(at * chunk, chunk), chunk)
            target[span, :] = source[span, :].astype(kind)
            return carry

        lax.fori_loop(0, count // chunk, one, 0)

    if mode == "fwd":
        def clear(at, carry):
            wide[pl.ds(pl.multiple_of(at * 512, 512), 512), :] = jnp.zeros((512, wide.shape[1]), F32)
            return carry

        lax.fori_loop(0, 2 * extent // 512, clear, 0)

    for copy in in_copies:
        copy.wait()

    if mode in ("fwd", "top"):
        solved = rowwise(inverse, inverse_copies, full).astype(BF16).astype(F32)
        if mode == "fwd":
            solved_ref[...] = solved.astype(BF16)
        vector_t = solved.T.astype(BF16)
    else:
        convert(full, wide, 2 * extent, F32)

        def pick(at, carry):
            base = pl.multiple_of(at * unroll, unroll)
            for offset in range(unroll):
                slot = slot_ref[base + offset]
                narrow[pl.ds(base + offset, 1), :] = wide[pl.ds(slot, 1), :]
            return carry

        lax.fori_loop(0, extent // unroll, pick, 0)
        convert(narrow, picked, extent, BF16)
        correction = rowwise(update, update_copies, picked)
        target = (prior_ref[...].astype(F32) - correction).astype(BF16).astype(F32)
        vector_t = target.T.astype(BF16)

    if mode == "fwd":
        def store_narrow(start, value):
            narrow[pl.ds(start, mul_width), :] = value

        colwise(vector_t, update, update_copies, store_narrow)

        def spread(at, carry):
            base = pl.multiple_of(at * unroll, unroll)
            for offset in range(unroll):
                slot = slot_ref[base + offset]
                wide[pl.ds(slot, 1), :] = narrow[pl.ds(base + offset, 1), :]
            return carry

        lax.fori_loop(0, extent // unroll, spread, 0)
        convert(wide, result, 2 * extent, BF16)
    else:
        def store_result(start, value):
            result[pl.ds(start, mul_width), :] = value.astype(BF16)

        colwise(vector_t, inverse, inverse_copies if mode == "back" else None, store_result)

    out_copies = []
    for swap, out_refs in ((1, sent_refs), (0, kept_refs)):
        for keys, out_ref in zip(groups, out_refs):
            for at, (leaf_diff, step) in enumerate(keys):
                index = block_index(place_out, depth, leaf_diff, step, swap)
                source = result.at[pl.ds(pl.multiple_of(index * rows, rows), rows), :]
                copy = pltpu.make_async_copy(source, out_ref.at[at], out_sem.at[len(out_copies)])
                copy.start()
                out_copies.append(copy)
    for copy in out_copies:
        copy.wait()


def run_level(mode, level, blocks, inverse, update=None, slots=None, prior=None):
    rows, extent = inverse.shape
    depth = lax.axis_size("panel") // CORES
    some = next(iter(blocks.values()))
    vec = some.shape[1]
    bits_in = {"fwd": level, "top": level, "back": level + 1}[mode]
    bits_out = {"fwd": level + 1, "top": level, "back": level}[mode]
    keys_in = list(blocks)
    groups = scatter_groups(bits_out, depth)
    size_in = len(keys_in) * rows
    size_out = sum(len(keys) for keys in groups) * CORES * rows
    load_width = widths(extent, 3072)
    plan = dict(
        bits_in=bits_in, bits_out=bits_out, depth=depth, mode=mode, keys_in=keys_in, groups=groups,
        rows=rows, extent=extent, load_width=load_width, mul_width=widths(extent, 512),
    )
    any_spec = pl.BlockSpec(memory_space=pl.ANY)
    operands, in_specs = [], []
    if mode != "top":
        operands.append(slots)
        in_specs.append(pl.BlockSpec(memory_space=pltpu.SMEM))
    for key in keys_in:
        operands.append(blocks[key])
        in_specs.append(any_spec)
    operands.append(inverse)
    in_specs.append(any_spec)
    if mode != "top":
        operands.append(update)
        in_specs.append(any_spec)
    if mode == "back":
        operands.append(prior)
        in_specs.append(pl.BlockSpec(memory_space=pltpu.VMEM))
    out_shape, out_specs = [], []
    if mode == "fwd":
        out_shape.append(jax.ShapeDtypeStruct((rows, vec), BF16))
        out_specs.append(pl.BlockSpec(memory_space=pltpu.VMEM))
    for _ in range(2):
        for keys in groups:
            out_shape.append(jax.ShapeDtypeStruct((len(keys), rows, vec), BF16))
            out_specs.append(any_spec)
    scratch = [pltpu.VMEM((size_in, vec), BF16), pltpu.VMEM((rows, extent), BF16)]
    if mode != "top":
        scratch += [
            pltpu.VMEM((rows, extent), BF16),
            pltpu.VMEM((2 * extent, vec), F32),
            pltpu.VMEM((extent, vec), F32),
        ]
    if mode == "back":
        scratch.append(pltpu.VMEM((extent, vec), BF16))
    scratch.append(pltpu.VMEM((size_out, vec), BF16))
    loads = extent // load_width
    scratch += [
        pltpu.SemaphoreType.DMA((len(keys_in),)),
        pltpu.SemaphoreType.DMA((loads,)),
        pltpu.SemaphoreType.DMA((loads,)),
        pltpu.SemaphoreType.DMA((size_out // rows,)),
    ]
    outs = pl.pallas_call(
        functools.partial(kernel_body, plan),
        out_shape=out_shape,
        in_specs=in_specs,
        out_specs=out_specs,
        scratch_shapes=scratch,
        compiler_params=pltpu.CompilerParams(vmem_limit_bytes=48 * 2**20),
        name=f"{mode}_{level}",
    )(*operands)
    outs = list(outs)
    solved = outs.pop(0) if mode == "fwd" else None
    count = len(groups)
    return solved, outs[:count], outs[count:]


def on_device(
    right_sides, inverse_low, inverse_mid, inverse_top, update_low, update_mid, slots_low, slots_mid
):
    inverses = (inverse_low, inverse_mid, inverse_top)
    updates = (update_low, update_mid)
    lists = (slots_low, slots_mid)
    height = len(inverses)
    leaf_at = lax.axis_index("leaf")
    slot_rows = [
        lax.dynamic_index_in_dim(lists[level], leaf_at >> level, 0, keepdims=False)
        for level in range(height - 1)
    ]
    solved = []
    local_rows = right_sides[0]
    for level in range(height - 1):
        blocks = gather_blocks(local_rows, level)
        done, kept, sent = run_level(
            "fwd", level, blocks, inverses[level], updates[level], slot_rows[level]
        )
        solved.append(done)
        carried = reduce_blocks(kept, sent, level + 1)
        local_rows = (right_sides[level + 1].astype(F32) - carried).astype(BF16)
    top = height - 1
    blocks = gather_blocks(local_rows, top)
    _, kept, sent = run_level("top", top, blocks, inverses[top])
    results = [None] * height
    results[top] = reduce_blocks(kept, sent, top).astype(BF16)
    for level in reversed(range(top)):
        blocks = gather_blocks(results[level + 1], level + 1)
        _, kept, sent = run_level(
            "back", level, blocks, inverses[level], updates[level], slot_rows[level], solved[level]
        )
        results[level] = reduce_blocks(kept, sent, level).astype(BF16)
    return jnp.stack(results)


def solution(mesh):
    both = ("leaf", "panel")
    return jax.shard_map(
        on_device,
        mesh=mesh,
        in_specs=(P(None, both, None),) + (P(both, None),) * 5 + (P(), P()),
        out_specs=P(None, both, None),
        check_vma=False,
    )
```

```python
import functools

import jax
import jax.numpy as jnp
from jax import lax
from jax.experimental import pallas as pl
from jax.experimental.pallas import tpu as pltpu
from jax.sharding import PartitionSpec as P


MUL = 1536
AXES = ("leaf", "panel")
CORES = 2
F32 = jnp.float32
BF16 = jnp.bfloat16


def swap_leaf(value, bit_at):
    leaves, panels = lax.axis_size("leaf"), lax.axis_size("panel")
    pairs = [
        (leaf * panels + at, (leaf ^ 1 << bit_at) * panels + at)
        for leaf in range(leaves)
        for at in range(panels)
    ]
    return lax.ppermute(value, AXES, pairs)


def swap_core(value):
    count = lax.axis_size("leaf") * lax.axis_size("panel")
    return lax.ppermute(value, AXES, [(i, i ^ 1) for i in range(count)])


def shift_depth(value, step):
    leaves, panels = lax.axis_size("leaf"), lax.axis_size("panel")
    depth = panels // CORES
    pairs = []
    for leaf in range(leaves):
        for at in range(panels):
            z, core = divmod(at, CORES)
            pairs.append((leaf * panels + at, leaf * panels + (z + step) % depth * CORES + core))
    return lax.ppermute(value, AXES, pairs)


def gather_blocks(block, bits):
    depth = lax.axis_size("panel") // CORES
    held = {(0, 0): block}
    for step in range(1, depth):
        held[0, step] = shift_depth(block, step)
    if bits >= 1:
        for step in range(depth):
            held[1, step] = swap_leaf(held[0, step], 0)
    if bits >= 2:
        for step in range(depth):
            held[2, step] = swap_leaf(held[0, step], 1)
            if step % 2:
                held[3, step] = swap_leaf(held[1, step], 1)
            else:
                held[3, step] = swap_leaf(held[2, step], 0)
    blocks = {}
    for (leaf_diff, step), value in held.items():
        blocks[leaf_diff, step, 0] = value
        blocks[leaf_diff, step, 1] = swap_core(value)
    return blocks


def add(*values):
    total = values[0].astype(F32)
    for value in values[1:]:
        total = total + value.astype(F32)
    return total


def scatter_groups(bits, depth):
    groups = []
    for even in reversed(range(0, depth, 2)):
        steps = [step for step in (even, even + 1) if step < depth]
        if bits == 0:
            groups.append([(0, step) for step in steps])
        elif bits == 1:
            groups.append([(1, step) for step in steps] + [(0, step) for step in steps])
        else:
            keys = [(3, even), (1, even)]
            if even + 1 < depth:
                keys += [(3, even + 1), (2, even + 1)]
            keys.append((2, even))
            if even + 1 < depth:
                keys.append((1, even + 1))
            groups.append(keys + [(0, step) for step in steps])
    return groups


def reduce_blocks(kept, sent, bits):
    depth = lax.axis_size("panel") // CORES
    groups = scatter_groups(bits, depth)
    base = {}
    for keys, mine, other in zip(groups, kept, sent):
        received = swap_core(other)
        part = lambda lo, hi: add(mine[lo:hi], received[lo:hi])
        steps = [step for leaf_diff, step in keys if leaf_diff == 0]
        first = len(keys) - len(steps)
        count = len(steps)
        if bits == 0:
            for at, step in enumerate(steps):
                base[step] = part(at, at + 1)
        elif bits == 1:
            via = swap_leaf(part(0, count).astype(BF16), 0)
            for at, step in enumerate(steps):
                base[step] = add(part(first + at, first + at + 1), via[at : at + 1])
        else:
            low = swap_leaf(part(0, 2).astype(BF16), 0)
            if count == 2:
                high = swap_leaf(part(2, 4).astype(BF16), 1)
            at = 2 * count
            next_low = swap_leaf(add(part(at, at + 1), low[:1]).astype(BF16), 1)
            base[steps[0]] = add(part(first, first + 1), low[1:2], next_low)
            if count == 2:
                next_high = swap_leaf(add(part(at + 1, at + 2), high[:1]).astype(BF16), 0)
                base[steps[1]] = add(part(first + 1, first + 2), high[1:2], next_high)
    order = [step for step in base if step]
    arrived = [shift_depth(base[step].astype(BF16), step) for step in order]
    return add(base[0], *arrived)[0]


def own_place(bits, depth):
    leaf = lax.axis_index("leaf") & (2**bits - 1)
    panel = lax.axis_index("panel")
    return leaf, panel // CORES, panel % CORES


def block_index(place, depth, leaf_diff, step, swap):
    leaf, z, core = place
    return ((leaf ^ leaf_diff) * depth + lax.rem(z + step + depth, depth)) * CORES + (core ^ swap)


def widths(extent, most):
    best = 128
    for width in range(128, most + 1, 128):
        if extent % width == 0:
            best = width
    return best


def kernel_body(plan, *refs):
    mode, depth, keys_in, groups = plan["mode"], plan["depth"], plan["keys_in"], plan["groups"]
    rows, extent = plan["rows"], plan["extent"]
    load_width, mul_width = plan["load_width"], plan["mul_width"]
    refs = list(refs)
    take = lambda count: [refs.pop(0) for _ in range(count)]
    slot_ref = take(1)[0] if mode != "top" else None
    block_refs = take(len(keys_in))
    inverse_ref = take(1)[0]
    update_ref = take(1)[0] if mode != "top" else None
    prior_ref = take(1)[0] if mode == "back" else None
    solved_ref = take(1)[0] if mode == "fwd" else None
    kept_refs = take(len(groups))
    sent_refs = take(len(groups))
    inverse = take(1)[0]
    update, wide, narrow = take(3) if mode != "top" else (None, None, None)
    gathered = take(1)[0]
    result = take(1)[0] if mode != "fwd" else None
    inverse_sem, update_sem = take(2)
    place_in = own_place(plan["bits_in"], depth)
    place_out = own_place(plan["bits_out"], depth)

    def start_weights(source, target, sem):
        copies = []
        for at in range(extent // load_width):
            cols = pl.ds(at * load_width, load_width)
            copy = pltpu.make_async_copy(source.at[:, cols], target.at[:, cols], sem.at[at])
            copy.start()
            copies.append(copy)
        return copies

    if mode == "back":
        update_copies = start_weights(update_ref, update, update_sem)
        inverse_copies = start_weights(inverse_ref, inverse, inverse_sem)
    else:
        inverse_copies = start_weights(inverse_ref, inverse, inverse_sem)
        update_copies = start_weights(update_ref, update, update_sem) if mode == "fwd" else None

    def span_of(place, leaf_diff, step, swap):
        index = block_index(place, depth, leaf_diff, step, swap)
        return pl.ds(pl.multiple_of(index * rows, rows), rows)

    assembled = wide if mode == "back" else gathered
    for block_ref, (leaf_diff, step, swap) in zip(block_refs, keys_in):
        block = block_ref[...]
        assembled[span_of(place_in, leaf_diff, -step, swap), :] = block.astype(assembled.dtype)

    def rowwise(matrix, copies, vector):
        total = None
        for at in range(extent // load_width):
            copies[at].wait()
            cols = pl.ds(at * load_width, load_width)
            term = jnp.dot(matrix[:, cols], vector[cols, :], preferred_element_type=F32)
            total = term if total is None else total + term
        return total

    def colwise(vector_t, matrix, copies, target):
        if copies is not None:
            for copy in copies:
                copy.wait()

        def one(at, carry):
            span = pl.ds(pl.multiple_of(at * mul_width, mul_width), mul_width)
            product = jnp.dot(vector_t, matrix[:, span], preferred_element_type=F32)
            target[span, :] = product.astype(BF16).T.astype(target.dtype)
            return carry

        lax.fori_loop(0, extent // mul_width, one, 0)

    def over(count, chunk, body):
        def one(at, carry):
            body(pl.multiple_of(at * chunk, chunk))
            return carry

        lax.fori_loop(0, count // chunk, one, 0)

    unroll = 64
    if mode == "fwd":
        def clear(start):
            wide[pl.ds(start, 1024), :] = jnp.zeros((1024, wide.shape[1]), F32)

        over(2 * extent, 1024, clear)
    if mode == "back":
        def pick(start):
            for offset in range(unroll):
                slot = slot_ref[start + offset]
                narrow[pl.ds(start + offset, 1), :] = wide[pl.ds(slot, 1), :]

        over(extent, unroll, pick)

        def cast(start):
            gathered[pl.ds(start, 1024), :] = narrow[pl.ds(start, 1024), :].astype(BF16)

        over(extent, 1024, cast)
        correction = rowwise(update, update_copies, gathered)
        vector = (prior_ref[...].astype(F32) - correction).astype(BF16)
    else:
        vector = rowwise(inverse, inverse_copies, gathered).astype(BF16)
    if mode == "fwd":
        solved_ref[...] = vector
    vector_t = vector.T
    if mode == "fwd":
        colwise(vector_t, update, update_copies, narrow)

        def spread(start):
            for offset in range(unroll):
                slot = slot_ref[start + offset]
                wide[pl.ds(slot, 1), :] = narrow[pl.ds(start + offset, 1), :]

        over(extent, unroll, spread)
        result = wide
    else:
        colwise(vector_t, inverse, inverse_copies if mode == "back" else None, result)
    for swap, out_refs in ((1, sent_refs), (0, kept_refs)):
        for keys, out_ref in zip(groups, out_refs):
            for at, (leaf_diff, step) in enumerate(keys):
                out_ref[at] = result[span_of(place_out, leaf_diff, step, swap), :].astype(BF16)


def run_level(mode, level, blocks, inverse, update=None, slots=None, prior=None):
    rows, extent = inverse.shape
    depth = lax.axis_size("panel") // CORES
    vec = next(iter(blocks.values())).shape[1]
    bits_in = {"fwd": level, "top": level, "back": level + 1}[mode]
    bits_out = {"fwd": level + 1, "top": level, "back": level}[mode]
    keys_in = list(blocks)
    groups = scatter_groups(bits_out, depth)
    load_width = widths(extent, 3072)
    plan = dict(
        bits_in=bits_in, bits_out=bits_out, depth=depth, mode=mode, keys_in=keys_in,
        groups=groups, rows=rows, extent=extent, load_width=load_width, mul_width=widths(extent, MUL),
    )
    any_spec = pl.BlockSpec(memory_space=pl.ANY)
    vmem_spec = pl.BlockSpec(memory_space=pltpu.VMEM)
    operands, in_specs = [], []
    if mode != "top":
        operands.append(slots)
        in_specs.append(pl.BlockSpec(memory_space=pltpu.SMEM))
    for key in keys_in:
        operands.append(blocks[key])
        in_specs.append(vmem_spec)
    operands.append(inverse)
    in_specs.append(any_spec)
    if mode != "top":
        operands.append(update)
        in_specs.append(any_spec)
    if mode == "back":
        operands.append(prior)
        in_specs.append(vmem_spec)
    out_shape = []
    if mode == "fwd":
        out_shape.append(jax.ShapeDtypeStruct((rows, vec), BF16))
    for keys in groups * 2:
        out_shape.append(jax.ShapeDtypeStruct((len(keys), rows, vec), BF16))
    scratch = [pltpu.VMEM((rows, extent), BF16)]
    if mode != "top":
        scratch += [
            pltpu.VMEM((rows, extent), BF16),
            pltpu.VMEM((2 * extent, vec), F32),
            pltpu.VMEM((extent, vec), F32),
        ]
    scratch.append(pltpu.VMEM((extent, vec), BF16))
    if mode != "fwd":
        scratch.append(pltpu.VMEM((extent, vec), BF16))
    scratch += [pltpu.SemaphoreType.DMA((extent // load_width,))] * 2
    outs = pl.pallas_call(
        functools.partial(kernel_body, plan),
        out_shape=out_shape,
        in_specs=in_specs,
        out_specs=[vmem_spec] * len(out_shape),
        scratch_shapes=scratch,
        compiler_params=pltpu.CompilerParams(vmem_limit_bytes=48 * 2**20),
        name=f"{mode}_{level}",
    )(*operands)
    outs = list(outs)
    solved = outs.pop(0) if mode == "fwd" else None
    return solved, outs[: len(groups)], outs[len(groups) :]


def on_device(
    right_sides, inverse_low, inverse_mid, inverse_top, update_low, update_mid, slots_low, slots_mid
):
    inverses = (inverse_low, inverse_mid, inverse_top)
    updates = (update_low, update_mid)
    lists = (slots_low, slots_mid)
    height = len(inverses)
    leaf_at = lax.axis_index("leaf")
    slot_rows = [
        lax.dynamic_index_in_dim(lists[level], leaf_at >> level, 0, keepdims=False)
        for level in range(height - 1)
    ]
    solved = []
    local_rows = right_sides[0]
    for level in range(height - 1):
        blocks = gather_blocks(local_rows, level)
        done, kept, sent = run_level(
            "fwd", level, blocks, inverses[level], updates[level], slot_rows[level]
        )
        solved.append(done)
        carried = reduce_blocks(kept, sent, level + 1)
        local_rows = (right_sides[level + 1].astype(F32) - carried).astype(BF16)
    top = height - 1
    blocks = gather_blocks(local_rows, top)
    _, kept, sent = run_level("top", top, blocks, inverses[top])
    results = [None] * height
    results[top] = reduce_blocks(kept, sent, top).astype(BF16)
    for level in reversed(range(top)):
        blocks = gather_blocks(results[level + 1], level + 1)
        _, kept, sent = run_level(
            "back", level, blocks, inverses[level], updates[level], slot_rows[level], solved[level]
        )
        results[level] = reduce_blocks(kept, sent, level).astype(BF16)
    return jnp.stack(results)


def solution(mesh):
    both = ("leaf", "panel")
    return jax.shard_map(
        on_device,
        mesh=mesh,
        in_specs=(P(None, both, None),) + (P(both, None),) * 5 + (P(), P()),
        out_specs=P(None, both, None),
        check_vma=False,
    )
```

```python
import functools
import math

import jax
import jax.numpy as jnp
from jax import lax
from jax.experimental import pallas as pl
from jax.experimental.pallas import tpu as pltpu
from jax.sharding import PartitionSpec as P


MUL = 1536
AXES = ("leaf", "panel")
CORES = 2
F32 = jnp.float32
BF16 = jnp.bfloat16


def swap_leaf(value, bit_at):
    leaves, panels = lax.axis_size("leaf"), lax.axis_size("panel")
    pairs = [
        (leaf * panels + at, (leaf ^ 1 << bit_at) * panels + at)
        for leaf in range(leaves)
        for at in range(panels)
    ]
    return lax.ppermute(value, AXES, pairs)


def swap_core(value):
    count = lax.axis_size("leaf") * lax.axis_size("panel")
    return lax.ppermute(value, AXES, [(i, i ^ 1) for i in range(count)])


def shift_depth(value, step):
    leaves, panels = lax.axis_size("leaf"), lax.axis_size("panel")
    depth = panels // CORES
    pairs = []
    for leaf in range(leaves):
        for at in range(panels):
            z, core = divmod(at, CORES)
            pairs.append((leaf * panels + at, leaf * panels + (z + step) % depth * CORES + core))
    return lax.ppermute(value, AXES, pairs)


def gather_blocks(block, bits):
    depth = lax.axis_size("panel") // CORES
    held = {(0, 0): block}
    for step in range(1, depth):
        held[0, step] = shift_depth(block, step)
    if bits >= 1:
        for step in range(depth):
            held[1, step] = swap_leaf(held[0, step], 0)
    if bits >= 2:
        for step in range(depth):
            held[2, step] = swap_leaf(held[0, step], 1)
            if step % 2:
                held[3, step] = swap_leaf(held[1, step], 1)
            else:
                held[3, step] = swap_leaf(held[2, step], 0)
    arrays = []
    for (leaf_diff, step), value in held.items():
        arrays.append((value, [(leaf_diff, step, 0)]))
        arrays.append((swap_core(value), [(leaf_diff, step, 1)]))
    return arrays


def add(*values):
    total = values[0].astype(F32)
    for value in values[1:]:
        total = total + value.astype(F32)
    return total


def scatter_groups(bits, depth):
    groups = []
    for even in reversed(range(0, depth, 2)):
        steps = [step for step in (even, even + 1) if step < depth]
        if bits == 0:
            groups.append([(0, step) for step in steps])
        elif bits == 1:
            groups.append([(1, step) for step in steps] + [(0, step) for step in steps])
        else:
            keys = [(3, even), (1, even)]
            if even + 1 < depth:
                keys += [(3, even + 1), (2, even + 1)]
            keys.append((2, even))
            if even + 1 < depth:
                keys.append((1, even + 1))
            groups.append(keys + [(0, step) for step in steps])
    return groups


def reduce_blocks(kept, sent, bits):
    depth = lax.axis_size("panel") // CORES
    groups = scatter_groups(bits, depth)
    base = {}
    for keys, mine, other in zip(groups, kept, sent):
        steps = [step for leaf_diff, step in keys if leaf_diff == 0]
        received = swap_core(other)
        part = lambda lo, hi: add(mine[lo:hi], received[lo:hi])
        first = len(keys) - len(steps)
        count = len(steps)
        if bits == 0:
            for at, step in enumerate(steps):
                base[step] = part(at, at + 1)
        elif bits == 1:
            via = swap_leaf(part(0, count).astype(BF16), 0)
            for at, step in enumerate(steps):
                base[step] = add(part(first + at, first + at + 1), via[at : at + 1])
        else:
            low = swap_leaf(part(0, 2).astype(BF16), 0)
            if count == 2:
                high = swap_leaf(part(2, 4).astype(BF16), 1)
            at = 2 * count
            next_low = swap_leaf(add(part(at, at + 1), low[:1]).astype(BF16), 1)
            base[steps[0]] = add(part(first, first + 1), low[1:2], next_low)
            if count == 2:
                next_high = swap_leaf(add(part(at + 1, at + 2), high[:1]).astype(BF16), 0)
                base[steps[1]] = add(part(first + 1, first + 2), high[1:2], next_high)
    order = [step for step in base if step]
    arrived = []
    for step in order:
        arrived.append(shift_depth(base[step].astype(BF16), step))
    return add(base[0], *arrived)[0]


def own_place(bits):
    leaf = lax.axis_index("leaf") & (2**bits - 1)
    panel = lax.axis_index("panel")
    return leaf, panel // CORES, panel % CORES


def block_index(place, depth, leaf_diff, step, swap):
    leaf, z, core = place
    return ((leaf ^ leaf_diff) * depth + lax.rem(z + step + depth, depth)) * CORES + (core ^ swap)


def widths(extent, most):
    best = 128
    for width in range(128, most + 1, 128):
        if extent % width == 0:
            best = width
    return best


def kernel_body(plan, *refs):
    mode, depth, keys_in, groups = plan["mode"], plan["depth"], plan["keys_in"], plan["groups"]
    rows, extent = plan["rows"], plan["extent"]
    load_width, mul_width = plan["load_width"], plan["mul_width"]
    refs = list(refs)
    take = lambda count: [refs.pop(0) for _ in range(count)]
    slot_ref = take(1)[0] if mode != "top" else None
    block_refs = take(len(keys_in))
    inverse_ref = take(1)[0]
    update_ref = take(1)[0] if mode != "top" else None
    prior_ref = take(1)[0] if mode == "back" else None
    solved_ref = take(1)[0] if mode == "fwd" else None
    kept_refs = take(len(groups))
    sent_refs = take(len(groups))
    inverse, update = (inverse_ref, update_ref) if plan["near"] else take(2)
    wide, narrow = take(2) if mode != "top" else (None, None)
    gathered = take(1)[0]
    result = take(1)[0] if mode != "fwd" else None
    weight_sem = None if plan["near"] else take(1)[0]
    place_in = own_place(plan["bits_in"])
    place_out = own_place(plan["bits_out"])

    def start(source, target, at):
        copies = []
        for half in range(2):
            span = pl.ds(half * (rows // 2), rows // 2)
            copy = pltpu.make_async_copy(
                source.at[span, :], target.at[span, :], weight_sem.at[2 * at + half]
            )
            copy.start()
            copies.append(copy)
        return copies

    def finish(copies):
        for copy in copies:
            copy.wait()

    update_copies, inverse_copies = [], []
    if not plan["near"]:
        if mode == "back":
            update_copies = start(update_ref, update, 0)
        inverse_copies = start(inverse_ref, inverse, 1)
        if mode == "fwd":
            update_copies = start(update_ref, update, 0)

    def span_of(place, leaf_diff, step, swap):
        index = block_index(place, depth, leaf_diff, step, swap)
        return pl.ds(pl.multiple_of(index * rows, rows), rows)

    assembled = wide if mode == "back" else gathered
    for block_ref, keys in zip(block_refs, keys_in):
        for at, (leaf_diff, step, swap) in enumerate(keys):
            block = block_ref[at * rows : (at + 1) * rows, :]
            assembled[span_of(place_in, leaf_diff, -step, swap), :] = block.astype(assembled.dtype)

    def rowwise(matrix, vector):
        total = None
        for at in range(extent // load_width):
            cols = pl.ds(at * load_width, load_width)
            term = jnp.dot(matrix[:, cols], vector[cols, :], preferred_element_type=F32)
            total = term if total is None else total + term
        return total

    def colwise(vector_t, matrix, target):
        def one(at, carry):
            span = pl.ds(pl.multiple_of(at * mul_width, mul_width), mul_width)
            product = jnp.dot(vector_t, matrix[:, span], preferred_element_type=F32)
            target[span, :] = product.astype(BF16).T.astype(target.dtype)
            return carry

        lax.fori_loop(0, extent // mul_width, one, 0)

    def over(count, chunk, body):
        def one(at, carry):
            body(pl.multiple_of(at * chunk, chunk))
            return carry

        lax.fori_loop(0, count // chunk, one, 0)

    unroll = 64
    if mode == "fwd":
        def clear(start):
            wide[pl.ds(start, 1024), :] = jnp.zeros((1024, wide.shape[1]), F32)

        over(2 * extent, 1024, clear)
    if mode == "back":
        def pick(start):
            for offset in range(unroll):
                slot = slot_ref[start + offset]
                narrow[pl.ds(start + offset, 1), :] = wide[pl.ds(slot, 1), :]

        over(extent, unroll, pick)

        def cast(start):
            gathered[pl.ds(start, 1024), :] = narrow[pl.ds(start, 1024), :].astype(BF16)

        over(extent, 1024, cast)
        finish(update_copies)
        correction = rowwise(update, gathered)
        vector = (prior_ref[...].astype(F32) - correction).astype(BF16)
    else:
        finish(inverse_copies)
        vector = rowwise(inverse, gathered).astype(BF16)
    if mode == "fwd":
        solved_ref[...] = vector
    vector_t = vector.T
    if mode == "fwd":
        finish(update_copies)
        colwise(vector_t, update, narrow)

        def spread(start):
            for offset in range(unroll):
                slot = slot_ref[start + offset]
                wide[pl.ds(slot, 1), :] = narrow[pl.ds(start + offset, 1), :]

        over(extent, unroll, spread)
        result = wide
    else:
        if mode == "back":
            finish(inverse_copies)
        colwise(vector_t, inverse, result)
    for swap, out_refs in ((1, sent_refs), (0, kept_refs)):
        for keys, out_ref in zip(groups, out_refs):
            for at, (leaf_diff, step) in enumerate(keys):
                out_ref[at] = result[span_of(place_out, leaf_diff, step, swap), :].astype(BF16)


def load_kernel(count, *refs):
    sources, targets, sem = refs[:count], refs[count + 1 : 2 * count + 1], refs[-1]
    copies = []
    for at, (source, target) in enumerate(zip(sources, targets)):
        rows = source.shape[0] // 2
        for half in range(2):
            span = pl.ds(half * rows, rows)
            copy = pltpu.make_async_copy(
                source.at[span, :], target.at[span, :], sem.at[2 * at + half]
            )
            copy.start()
            copies.append(copy)
    for copy in copies:
        copy.wait()


def load(matrices, after):
    hbm_spec = pl.BlockSpec(memory_space=pltpu.MemorySpace.HBM)
    vmem_spec = pl.BlockSpec(memory_space=pltpu.VMEM)
    count = len(matrices)
    size = sum(math.prod(m.shape) * m.dtype.itemsize for m in matrices)
    out_shape = [jax.ShapeDtypeStruct(m.shape, m.dtype) for m in matrices]
    matrices = [pltpu.with_memory_space_constraint(m, pltpu.MemorySpace.HBM) for m in matrices]
    return pl.pallas_call(
        functools.partial(load_kernel, count),
        out_shape=out_shape,
        in_specs=[hbm_spec] * count + [pl.BlockSpec(memory_space=pl.ANY)],
        out_specs=[vmem_spec] * count,
        scratch_shapes=[pltpu.SemaphoreType.DMA((2 * count,))],
        compiler_params=pltpu.CompilerParams(vmem_limit_bytes=4 * 2**20),
        cost_estimate=pl.CostEstimate(flops=0, bytes_accessed=2 * size, transcendentals=0),
    )(*matrices, after)


def run_level(mode, level, blocks, inverse, update=None, slots=None, prior=None, near=False):
    rows, extent = inverse.shape
    depth = lax.axis_size("panel") // CORES
    vec = blocks[0][0].shape[1]
    bits_in = {"fwd": level, "top": level, "back": level + 1}[mode]
    bits_out = {"fwd": level + 1, "top": level, "back": level}[mode]
    keys_in = [keys for _, keys in blocks]
    groups = scatter_groups(bits_out, depth)
    load_width = widths(extent, 3072)
    plan = dict(
        near=near,
        bits_in=bits_in, bits_out=bits_out, depth=depth, mode=mode, keys_in=keys_in,
        groups=groups, rows=rows, extent=extent, load_width=load_width, mul_width=widths(extent, MUL),
    )
    vmem_spec = pl.BlockSpec(memory_space=pltpu.VMEM)
    operands, in_specs = [], []
    if mode != "top":
        operands.append(slots)
        in_specs.append(pl.BlockSpec(memory_space=pltpu.SMEM))
    for value, _ in blocks:
        operands.append(value)
        in_specs.append(vmem_spec)
    far_spec = pl.BlockSpec(memory_space=pltpu.MemorySpace.HBM)
    far = lambda value: pltpu.with_memory_space_constraint(value, pltpu.MemorySpace.HBM)
    for weights in (inverse, update):
        if weights is not None:
            operands.append(weights if near else far(weights))
            in_specs.append(vmem_spec if near else far_spec)
    if mode == "back":
        operands.append(prior)
        in_specs.append(vmem_spec)
    out_shape = []
    if mode == "fwd":
        out_shape.append(jax.ShapeDtypeStruct((rows, vec), BF16))
    for keys in groups * 2:
        out_shape.append(jax.ShapeDtypeStruct((len(keys), rows, vec), BF16))
    scratch = [] if near else [pltpu.VMEM((rows, extent), BF16)] * 2
    if mode != "top":
        scratch += [pltpu.VMEM((2 * extent, vec), F32), pltpu.VMEM((extent, vec), F32)]
    scratch.append(pltpu.VMEM((extent, vec), BF16))
    if mode != "fwd":
        scratch.append(pltpu.VMEM((extent, vec), BF16))
    held = sum(math.prod(ref.shape) * ref.dtype.itemsize for ref in scratch)
    if not near:
        scratch.append(pltpu.SemaphoreType.DMA((4,)))
    outs = pl.pallas_call(
        functools.partial(kernel_body, plan),
        out_shape=out_shape,
        in_specs=in_specs,
        out_specs=[vmem_spec] * len(out_shape),
        scratch_shapes=scratch,
        compiler_params=pltpu.CompilerParams(vmem_limit_bytes=held + 12 * 2**20),
    )(*operands)
    outs = list(outs)
    solved = outs.pop(0) if mode == "fwd" else None
    return solved, outs[: len(groups)], outs[len(groups) :]


def on_device(
    right_sides, inverse_low, inverse_mid, inverse_top, update_low, update_mid, slots_low, slots_mid
):
    inverses = (inverse_low, inverse_mid, inverse_top)
    updates = (update_low, update_mid)
    lists = (slots_low, slots_mid)
    height = len(inverses)
    leaf_at = lax.axis_index("leaf")
    slot_rows = [
        lax.dynamic_index_in_dim(lists[level], leaf_at >> level, 0, keepdims=False)
        for level in range(height - 1)
    ]
    solved = []
    local_rows = right_sides[0]
    for level in range(height - 1):
        inverse, update = inverses[level], updates[level]
        if level == 0:
            inverse, update = load((inverse, update), local_rows)
        blocks = gather_blocks(local_rows, level)
        done, kept, sent = run_level(
            "fwd", level, blocks, inverse, update, slot_rows[level], near=level == 0
        )
        solved.append(done)
        carried = reduce_blocks(kept, sent, level + 1)
        local_rows = (right_sides[level + 1].astype(F32) - carried).astype(BF16)
    top = height - 1
    (inverse,) = load((inverses[top],), local_rows)
    blocks = gather_blocks(local_rows, top)
    _, kept, sent = run_level("top", top, blocks, inverse, near=True)
    results = [None] * height
    results[top] = reduce_blocks(kept, sent, top).astype(BF16)
    for level in reversed(range(top)):
        inverse, update = load((inverses[level], updates[level]), results[level + 1])
        blocks = gather_blocks(results[level + 1], level + 1)
        _, kept, sent = run_level(
            "back", level, blocks, inverse, update, slot_rows[level], solved[level], near=True
        )
        results[level] = reduce_blocks(kept, sent, level).astype(BF16)
    return jnp.stack(results)


def solution(mesh):
    both = ("leaf", "panel")

    return jax.shard_map(
        on_device,
        mesh=mesh,
        in_specs=(P(None, both, None),) + (P(both, None),) * 5 + (P(), P()),
        out_specs=P(None, both, None),
        check_vma=False,
    )
```

```python
import functools
import math

import jax
import jax.numpy as jnp
from jax import lax
from jax.experimental import pallas as pl
from jax.experimental.pallas import tpu as pltpu
from jax.sharding import PartitionSpec as P


MUL = 1536
AXES = ("leaf", "panel")
CORES = 2
F32 = jnp.float32
BF16 = jnp.bfloat16


def swap_leaf(value, bit_at):
    leaves, panels = lax.axis_size("leaf"), lax.axis_size("panel")
    pairs = [
        (leaf * panels + at, (leaf ^ 1 << bit_at) * panels + at)
        for leaf in range(leaves)
        for at in range(panels)
    ]
    return lax.ppermute(value, AXES, pairs)


def swap_core(value):
    count = lax.axis_size("leaf") * lax.axis_size("panel")
    return lax.ppermute(value, AXES, [(i, i ^ 1) for i in range(count)])


def shift_depth(value, step):
    leaves, panels = lax.axis_size("leaf"), lax.axis_size("panel")
    depth = panels // CORES
    pairs = []
    for leaf in range(leaves):
        for at in range(panels):
            z, core = divmod(at, CORES)
            pairs.append((leaf * panels + at, leaf * panels + (z + step) % depth * CORES + core))
    return lax.ppermute(value, AXES, pairs)


def gather_blocks(block, bits):
    depth = lax.axis_size("panel") // CORES
    held = {(0, 0): block}
    for step in range(1, depth):
        held[0, step] = shift_depth(block, step)
    if bits >= 1:
        for step in range(depth):
            held[1, step] = swap_leaf(held[0, step], 0)
    if bits >= 2:
        for step in range(depth):
            held[2, step] = swap_leaf(held[0, step], 1)
            if step % 2:
                held[3, step] = swap_leaf(held[1, step], 1)
            else:
                held[3, step] = swap_leaf(held[2, step], 0)
    arrays = []
    for (leaf_diff, step), value in held.items():
        arrays.append((value, [(leaf_diff, step, 0)]))
        arrays.append((swap_core(value), [(leaf_diff, step, 1)]))
    return arrays


def add(*values):
    total = values[0].astype(F32)
    for value in values[1:]:
        total = total + value.astype(F32)
    return total


def scatter_groups(bits, depth):
    groups = []
    for even in reversed(range(0, depth, 2)):
        steps = [step for step in (even, even + 1) if step < depth]
        if bits == 0:
            groups.append([(0, step) for step in steps])
        elif bits == 1:
            groups.append([(1, step) for step in steps] + [(0, step) for step in steps])
        else:
            keys = [(3, even), (1, even)]
            if even + 1 < depth:
                keys += [(3, even + 1), (2, even + 1)]
            keys.append((2, even))
            if even + 1 < depth:
                keys.append((1, even + 1))
            groups.append(keys + [(0, step) for step in steps])
    return groups


def reduce_blocks(kept, sent, bits):
    depth = lax.axis_size("panel") // CORES
    groups = scatter_groups(bits, depth)
    base = {}
    for keys, mine, other in zip(groups, kept, sent):
        steps = [step for leaf_diff, step in keys if leaf_diff == 0]
        received = swap_core(other)
        part = lambda lo, hi: add(mine[lo:hi], received[lo:hi])
        first = len(keys) - len(steps)
        count = len(steps)
        if bits == 0:
            for at, step in enumerate(steps):
                base[step] = part(at, at + 1)
        elif bits == 1:
            via = swap_leaf(part(0, count).astype(BF16), 0)
            for at, step in enumerate(steps):
                base[step] = add(part(first + at, first + at + 1), via[at : at + 1])
        else:
            low = swap_leaf(part(0, 2).astype(BF16), 0)
            if count == 2:
                high = swap_leaf(part(2, 4).astype(BF16), 1)
            at = 2 * count
            next_low = swap_leaf(add(part(at, at + 1), low[:1]).astype(BF16), 1)
            base[steps[0]] = add(part(first, first + 1), low[1:2], next_low)
            if count == 2:
                next_high = swap_leaf(add(part(at + 1, at + 2), high[:1]).astype(BF16), 0)
                base[steps[1]] = add(part(first + 1, first + 2), high[1:2], next_high)
    order = [step for step in base if step]
    arrived = []
    for step in order:
        arrived.append(shift_depth(base[step].astype(BF16), step))
    return add(base[0], *arrived)[0]


def own_place(bits):
    leaf = lax.axis_index("leaf") & (2**bits - 1)
    panel = lax.axis_index("panel")
    return leaf, panel // CORES, panel % CORES


def block_index(place, depth, leaf_diff, step, swap):
    leaf, z, core = place
    return ((leaf ^ leaf_diff) * depth + lax.rem(z + step + depth, depth)) * CORES + (core ^ swap)


def widths(extent, most):
    best = 128
    for width in range(128, most + 1, 128):
        if extent % width == 0:
            best = width
    return best


def kernel_body(plan, *refs):
    mode, depth, keys_in, groups = plan["mode"], plan["depth"], plan["keys_in"], plan["groups"]
    rows, extent = plan["rows"], plan["extent"]
    load_width, mul_width = plan["load_width"], plan["mul_width"]
    refs = list(refs)
    take = lambda count: [refs.pop(0) for _ in range(count)]
    slot_ref = take(1)[0] if mode != "top" else None
    block_refs = take(len(keys_in))
    inverse_ref = take(1)[0]
    update_ref = take(1)[0] if mode != "top" else None
    prior_ref = take(1)[0] if mode == "back" else None
    solved_ref = take(1)[0] if mode == "fwd" else None
    kept_refs = take(len(groups))
    sent_refs = take(len(groups))
    inverse, update = (inverse_ref, update_ref) if plan["near"] else take(2)
    wide, narrow = take(2) if mode != "top" else (None, None)
    gathered = take(1)[0]
    result = take(1)[0] if mode != "fwd" else None
    weight_sem = None if plan["near"] else take(1)[0]
    place_in = own_place(plan["bits_in"])
    place_out = own_place(plan["bits_out"])

    def start(source, target, at):
        copies = []
        for half in range(2):
            span = pl.ds(half * (rows // 2), rows // 2)
            copy = pltpu.make_async_copy(
                source.at[span, :], target.at[span, :], weight_sem.at[2 * at + half]
            )
            copy.start()
            copies.append(copy)
        return copies

    def finish(copies):
        for copy in copies:
            copy.wait()

    update_copies, inverse_copies = [], []
    if not plan["near"]:
        if mode == "back":
            update_copies = start(update_ref, update, 0)
        inverse_copies = start(inverse_ref, inverse, 1)
        if mode == "fwd":
            update_copies = start(update_ref, update, 0)

    def span_of(place, leaf_diff, step, swap):
        index = block_index(place, depth, leaf_diff, step, swap)
        return pl.ds(pl.multiple_of(index * rows, rows), rows)

    assembled = wide if mode == "back" else gathered
    for block_ref, keys in zip(block_refs, keys_in):
        for at, (leaf_diff, step, swap) in enumerate(keys):
            block = block_ref[at * rows : (at + 1) * rows, :]
            assembled[span_of(place_in, leaf_diff, -step, swap), :] = block.astype(assembled.dtype)

    def rowwise(matrix, vector):
        total = None
        for at in range(extent // load_width):
            cols = pl.ds(at * load_width, load_width)
            term = jnp.dot(matrix[:, cols], vector[cols, :], preferred_element_type=F32)
            total = term if total is None else total + term
        return total

    def colwise(vector_t, matrix, target):
        def one(at, carry):
            span = pl.ds(pl.multiple_of(at * mul_width, mul_width), mul_width)
            product = jnp.dot(vector_t, matrix[:, span], preferred_element_type=F32)
            target[span, :] = product.astype(BF16).T.astype(target.dtype)
            return carry

        lax.fori_loop(0, extent // mul_width, one, 0)

    def over(count, chunk, body):
        def one(at, carry):
            body(pl.multiple_of(at * chunk, chunk))
            return carry

        lax.fori_loop(0, count // chunk, one, 0)

    unroll = 64
    if mode == "fwd":
        def clear(start):
            wide[pl.ds(start, 1024), :] = jnp.zeros((1024, wide.shape[1]), F32)

        over(2 * extent, 1024, clear)
    if mode == "back":
        def pick(start):
            for offset in range(unroll):
                slot = slot_ref[start + offset]
                narrow[pl.ds(start + offset, 1), :] = wide[pl.ds(slot, 1), :]

        over(extent, unroll, pick)

        def cast(start):
            gathered[pl.ds(start, 1024), :] = narrow[pl.ds(start, 1024), :].astype(BF16)

        over(extent, 1024, cast)
        finish(update_copies)
        correction = rowwise(update, gathered)
        vector = (prior_ref[...].astype(F32) - correction).astype(BF16)
    else:
        finish(inverse_copies)
        vector = rowwise(inverse, gathered).astype(BF16)
    if mode == "fwd":
        solved_ref[...] = vector
    vector_t = vector.T
    if mode == "fwd":
        finish(update_copies)
        colwise(vector_t, update, narrow)

        def spread(start):
            for offset in range(unroll):
                slot = slot_ref[start + offset]
                wide[pl.ds(slot, 1), :] = narrow[pl.ds(start + offset, 1), :]

        over(extent, unroll, spread)
        result = wide
    else:
        if mode == "back":
            finish(inverse_copies)
        colwise(vector_t, inverse, result)
    for swap, out_refs in ((1, sent_refs), (0, kept_refs)):
        for keys, out_ref in zip(groups, out_refs):
            for at, (leaf_diff, step) in enumerate(keys):
                out_ref[at] = result[span_of(place_out, leaf_diff, step, swap), :].astype(BF16)


def load_kernel(count, *refs):
    sources, targets, sem = refs[:count], refs[count + 1 : 2 * count + 1], refs[-1]
    copies = []
    for at, (source, target) in enumerate(zip(sources, targets)):
        rows = source.shape[0] // 2
        for half in range(2):
            span = pl.ds(half * rows, rows)
            copy = pltpu.make_async_copy(
                source.at[span, :], target.at[span, :], sem.at[2 * at + half]
            )
            copy.start()
            copies.append(copy)
    for copy in copies:
        copy.wait()


def load(matrices, after):
    hbm_spec = pl.BlockSpec(memory_space=pltpu.MemorySpace.HBM)
    vmem_spec = pl.BlockSpec(memory_space=pltpu.VMEM)
    count = len(matrices)
    size = sum(math.prod(m.shape) * m.dtype.itemsize for m in matrices)
    out_shape = [jax.ShapeDtypeStruct(m.shape, m.dtype) for m in matrices]
    matrices = [pltpu.with_memory_space_constraint(m, pltpu.MemorySpace.HBM) for m in matrices]
    return pl.pallas_call(
        functools.partial(load_kernel, count),
        out_shape=out_shape,
        in_specs=[hbm_spec] * count + [pl.BlockSpec(memory_space=pl.ANY)],
        out_specs=[vmem_spec] * count,
        scratch_shapes=[pltpu.SemaphoreType.DMA((2 * count,))],
        compiler_params=pltpu.CompilerParams(vmem_limit_bytes=4 * 2**20),
        cost_estimate=pl.CostEstimate(flops=0, bytes_accessed=2 * size, transcendentals=0),
    )(*matrices, after)


def run_level(mode, level, blocks, inverse, update=None, slots=None, prior=None, near=False):
    rows, extent = inverse.shape
    depth = lax.axis_size("panel") // CORES
    vec = blocks[0][0].shape[1]
    bits_in = {"fwd": level, "top": level, "back": level + 1}[mode]
    bits_out = {"fwd": level + 1, "top": level, "back": level}[mode]
    keys_in = [keys for _, keys in blocks]
    groups = scatter_groups(bits_out, depth)
    load_width = widths(extent, 3072)
    plan = dict(
        near=near,
        bits_in=bits_in, bits_out=bits_out, depth=depth, mode=mode, keys_in=keys_in,
        groups=groups, rows=rows, extent=extent, load_width=load_width, mul_width=widths(extent, MUL),
    )
    vmem_spec = pl.BlockSpec(memory_space=pltpu.VMEM)
    operands, in_specs = [], []
    if mode != "top":
        operands.append(slots)
        in_specs.append(pl.BlockSpec(memory_space=pltpu.SMEM))
    for value, _ in blocks:
        operands.append(value)
        in_specs.append(vmem_spec)
    far_spec = pl.BlockSpec(memory_space=pltpu.MemorySpace.HBM)
    far = lambda value: pltpu.with_memory_space_constraint(value, pltpu.MemorySpace.HBM)
    for weights in (inverse, update):
        if weights is not None:
            operands.append(weights if near else far(weights))
            in_specs.append(vmem_spec if near else far_spec)
    if mode == "back":
        operands.append(prior)
        in_specs.append(vmem_spec)
    out_shape = []
    if mode == "fwd":
        out_shape.append(jax.ShapeDtypeStruct((rows, vec), BF16))
    for keys in groups * 2:
        out_shape.append(jax.ShapeDtypeStruct((len(keys), rows, vec), BF16))
    scratch = [] if near else [pltpu.VMEM((rows, extent), BF16)] * 2
    if mode != "top":
        scratch += [pltpu.VMEM((2 * extent, vec), F32), pltpu.VMEM((extent, vec), F32)]
    scratch.append(pltpu.VMEM((extent, vec), BF16))
    if mode != "fwd":
        scratch.append(pltpu.VMEM((extent, vec), BF16))
    held = sum(math.prod(ref.shape) * ref.dtype.itemsize for ref in scratch)
    if not near:
        scratch.append(pltpu.SemaphoreType.DMA((4,)))
    outs = pl.pallas_call(
        functools.partial(kernel_body, plan),
        out_shape=out_shape,
        in_specs=in_specs,
        out_specs=[vmem_spec] * len(out_shape),
        scratch_shapes=scratch,
        compiler_params=pltpu.CompilerParams(vmem_limit_bytes=held + 12 * 2**20),
    )(*operands)
    outs = list(outs)
    solved = outs.pop(0) if mode == "fwd" else None
    return solved, outs[: len(groups)], outs[len(groups) :]


def on_device(
    right_sides, inverse_low, inverse_mid, inverse_top, update_low, update_mid, slots_low, slots_mid
):
    inverses = (inverse_low, inverse_mid, inverse_top)
    updates = (update_low, update_mid)
    lists = (slots_low, slots_mid)
    height = len(inverses)
    leaf_at = lax.axis_index("leaf")
    slot_rows = []
    for level in range(height - 1):
        slot_rows.append(
            lax.dynamic_index_in_dim(lists[level], leaf_at >> level, 0, keepdims=False)
        )
    solved = []
    local_rows = right_sides[0]
    for level in range(height - 1):
        inverse, update = inverses[level], updates[level]
        if level == 0:
            inverse, update = load((inverse, update), local_rows)
        blocks = gather_blocks(local_rows, level)
        done, kept, sent = run_level(
            "fwd", level, blocks, inverse, update, slot_rows[level], near=level == 0
        )
        solved.append(done)
        carried = reduce_blocks(kept, sent, level + 1)
        local_rows = (right_sides[level + 1].astype(F32) - carried).astype(BF16)
    top = height - 1
    (inverse,) = load((inverses[top],), local_rows)
    blocks = gather_blocks(local_rows, top)
    _, kept, sent = run_level("top", top, blocks, inverse, near=True)
    results = [None] * height
    results[top] = reduce_blocks(kept, sent, top).astype(BF16)
    for level in reversed(range(top)):
        inverse, update = load((inverses[level], updates[level]), results[level + 1])
        blocks = gather_blocks(results[level + 1], level + 1)
        _, kept, sent = run_level(
            "back", level, blocks, inverse, update, slot_rows[level], solved[level], near=True
        )
        results[level] = reduce_blocks(kept, sent, level).astype(BF16)
    return jnp.stack(results)


def solution(mesh):
    both = ("leaf", "panel")

    return jax.shard_map(
        on_device,
        mesh=mesh,
        in_specs=(P(None, both, None),) + (P(both, None),) * 5 + (P(), P()),
        out_specs=P(None, both, None),
        check_vma=False,
    )
```
